32 devices in a mesh: src: 8 (over z, y), rcv: 2 (over x), freq: 2 (over core).
Axes of the slice: x: 2, y: 2, z: 4, core: 2. Of those that a mesh axis runs over, the one named last changes fastest.
Arguments:
- recorded: float32 [2, 2, 4096, 4096], P('freq', None, 'src', 'rcv'), parts along dimension 0, as said below
Outputs:
- multiples: float32 [2, 2, 4096, 4096], P('freq', None, 'src', 'rcv'), parts along dimension 0
There are 2 independent parts, one for each index of `freq`. The reference program is written for one: setup_inputs(seed, part) draws one part's arguments, and reference() takes and returns one part's arrays. A program takes and returns all parts, laid end to end along the dimension named above; each array names one. Nothing has to cross between parts.
Inputs may be any that keep to these rules, and one draw needn't show every extreme that they name: By reciprocity each frequency bin's data is symmetric: recorded[f, c, s, r] equals recorded[f, c, r, s].
All inputs are finite; a program needn't handle non-finite values.
Results may differ from the reference program's by a relative error of at most 0.00007.
Values sent between devices are 32-bit elements; how exact they have to be, the bound alone decides.
No kernel may reach another device: no remote copies, remote signals or barrier semaphores. Data moves between devices by JAX's collectives and lax.ppermute only.
A program may use at most 192 MiB of HBM per device.

```python
import jax
import jax.numpy as jnp
from jax import lax

NS = 4096
FREQS = 1


def draw_recorded(key, part):
    scale = (4.0 * NS) ** (-0.25)
    base_key = jax.random.fold_in(jax.random.fold_in(key, 11), 0)
    values = jax.random.normal(base_key, (FREQS, 2, NS, NS), jnp.float32)
    symmetric = (values + jnp.swapaxes(values, 2, 3)) * 0.70710678
    return (symmetric * scale).astype(jnp.float32)


def setup_inputs(seed: int = 0, part: int = 0) -> dict:
    keys = jax.random.split(jax.random.key(seed), 2)
    part_keys = jax.random.split(jax.random.fold_in(keys[1], part), 2)
    recorded = draw_recorded(jax.random.fold_in(jax.random.fold_in(keys[1], part), 71), part)
    return {"recorded": recorded}


def complex_product(left, right):
    highest = lax.Precision.HIGHEST

    def multiply(first, second):
        return jnp.einsum("fik,fkj->fij", first, second, precision=highest)

    real_part = multiply(left[:, 0], right[:, 0]) - multiply(left[:, 1], right[:, 1])
    imag_part = multiply(left[:, 0], right[:, 1]) + multiply(left[:, 1], right[:, 0])
    return jnp.stack([real_part, imag_part], axis=1)


def reference(recorded):
    return complex_product(recorded, recorded)
```

```python
import functools
import random

import jax
import jax.numpy as jnp
import numpy as np
from jax import lax
from jax.experimental import pallas as pl
from jax.experimental.pallas import tpu as pltpu
from jax.sharding import PartitionSpec as P

AXES = ("src", "rcv")


def split_axis(n):
    return (n,) if n <= 4 else (4, n // 4)


class Grid:
    def __init__(self, src, rcv):
        self.src, self.rcv, self.width = src, rcv, src // rcv
        dims = split_axis(src) + split_axis(rcv)
        self.count = src * rcv
        place = np.array(np.unravel_index(np.arange(self.count), dims)).T
        self.dist = np.abs(place[:, None] - place[None]).sum(-1)
        self.ways = []
        for axis, size in enumerate(dims):
            for sign in (1, -1) if size > 2 else (0,):
                pairs = []
                for u in range(self.count):
                    to = place[u].copy()
                    to[axis] = 1 - to[axis] if sign == 0 else to[axis] + sign
                    if 0 <= to[axis] < size:
                        pairs.append((u, int(np.ravel_multi_index(tuple(to), dims))))
                if pairs:
                    self.ways.append(pairs)
        self.tiles = [(p, q) for p in range(src) for q in range(p, src)]
        self.number = {}
        for i, (p, q) in enumerate(self.tiles):
            self.number[p, q] = self.number[q, p] = i

    def columns(self, x):
        return range(x * self.width, (x + 1) * self.width)


def plan_moves(grid, seed):
    rnd = random.Random(seed)
    items, n = 2 * len(grid.tiles), grid.count
    has = np.full((n, items), 10**6)
    need = np.zeros((n, items), bool)
    row = np.zeros((n, items), bool)
    flip = np.zeros((n, items), bool)
    for d in range(n):
        s, x = divmod(d, grid.rcv)
        for c in range(2):
            for q in range(grid.src):
                need[d, 2 * grid.number[s, q] + c] = True
                row[d, 2 * grid.number[s, q] + c] = True
                for j in grid.columns(x):
                    need[d, 2 * grid.number[q, j] + c] = True
            for q in grid.columns(x):
                has[d, 2 * grid.number[s, q] + c] = 0
                flip[d, 2 * grid.number[s, q] + c] = s > q
    links = [(way, u, v) for way, pairs in enumerate(grid.ways) for u, v in pairs]
    degree = np.zeros(n)
    for _, _, v in links:
        degree[v] += 1
    near = np.stack([grid.dist[has[:, i] == 0].min(0) for i in range(items)])
    moves, step = [], 0
    while True:
        missing = need & (has > 10**5)
        if not missing.any():
            return moves, has, flip
        load = missing.sum(1) / degree
        weight = missing.sum(1) / np.maximum(need.sum(1), 1)
        rnd.shuffle(links)
        links.sort(key=lambda link: -load[link[2]])
        open_ = has > 10**5
        into = [[] for _ in range(n)]
        for _, u, v in links:
            into[v].append(u)
        ready = has <= step
        now = []
        for way, u, v in links:
            cand = np.nonzero(ready[u] & open_[v])[0]
            if not len(cand):
                continue
            helped = (missing[:, cand].T & (grid.dist[v][None] < near[cand])).astype(float)
            helped[:, v] = 0
            value = 3.0 * missing[v, cand] + helped @ weight
            useful = value > 0
            if not useful.any():
                continue
            others = sum(ready[w, cand].astype(float) for w in into[v])
            value = value + 0.5 * np.array([rnd.random() for _ in cand]) - 0.7 * (others - 1)
            value = value + 0.6 * (row[v, cand] & missing[v, cand])
            value[~useful] = -100
            item = int(cand[np.argmax(value)])
            open_[v, item] = False
            missing[v, item] = False
            near[item] = np.minimum(near[item], grid.dist[v])
            now.append((way, u, v, item))
        for _, u, v, item in now:
            has[v, item] = step + 2
            flip[v, item] = flip[u, item]
        moves.append(now)
        step += 1


@functools.lru_cache(None)
def plan(src, rcv):
    grid = Grid(src, rcv)
    best = None
    for seed in range(24 if grid.count <= 16 else 1):
        got = plan_moves(grid, seed)
        if best is None or len(got[0]) < len(best[0]):
            best = got
    moves, has, flip = best
    n, ways, steps = grid.count, len(grid.ways), len(moves)
    slot = np.full((n, 2 * len(grid.tiles)), -1)
    used = np.zeros(n, int)
    for d in range(n):
        s, x = divmod(d, rcv)
        for q in grid.columns(x):
            for c in range(2):
                slot[d, 2 * grid.number[s, q] + c] = used[d]
                used[d] += 1
    send = np.full((steps + 2, ways, n), -1)
    take = np.full((steps + 2, ways, n), -1)
    perms = [[[] for _ in range(ways)] for _ in range(steps)]
    for step, now in enumerate(moves):
        for way, u, v, item in now:
            slot[v, item] = used[v]
            used[v] += 1
            take[step + 2, way, v] = slot[v, item]
            perms[step][way].append((u, v))
    for step, now in enumerate(moves):
        taken = [way for way in range(ways) if step >= 2 and perms[step - 2][way]]
        for way, u, v, item in now:
            new = [i for i, w in enumerate(taken) if take[step, w, u] == slot[u, item]]
            send[step, way, u] = used.max() + new[0] if new else slot[u, item]
    calls = sorted({*range(4, steps, 2), *range(max(steps - 3, 0), steps + 2)})
    cap = 10
    lists = [[[] for _ in range(n)] for _ in calls]
    for d in range(n):
        s, x = divmod(d, rcv)
        todo = []
        for k in range(src):
            left = [2 * grid.number[s, k] + c for c in range(2)]
            for j, q in enumerate(grid.columns(x)):
                for c in range(2):
                    right = 2 * grid.number[k, q] + c
                    ready = max(has[d, left[0]], has[d, left[1]], has[d, right])
                    todo.append((ready, k, j, c, left, right, q))
        todo.sort()
        for at, step in enumerate(calls):
            fit = [one for one in todo if one[0] <= step]
            if step < steps + 1:
                fit = fit[:cap]
            todo = [one for one in todo if one not in fit]
            fit.sort(key=lambda one: one[1])
            old = None
            for ready, k, j, c, left, right, q in fit:
                lt = [int((s > k) != flip[d, i]) for i in left]
                rt = int((k > q) != flip[d, right])
                lists[at][d].append(
                    (slot[d, left[0]], slot[d, left[1]], lt[0], lt[1], int(k != old), slot[d, right], rt, j, c)
                )
                old = k
        assert not todo
    longest = [max(len(one) for one in per) for per in lists]
    table = []
    starts = {}
    for step in range(steps + 2):
        starts["route", step] = len(table)
        for way in range(ways):
            table.append(take[step, way])
        for way in range(ways):
            table.append(send[step, way])
    for at, step in enumerate(calls):
        starts["ops", step] = len(table)
        table.append(np.array([len(lists[at][d]) for d in range(n)]))
        for i in range(longest[at]):
            for f in range(9):
                table.append(np.array([lists[at][d][i][f] if i < len(lists[at][d]) else 0 for d in range(n)]))
    return perms, calls, longest, starts, np.array(table, np.int32).T.copy(), int(used.max()), ways


ANY = pl.BlockSpec(memory_space=pl.ANY)


def first_kernel(tab, own, buf, hold, sem):
    tile = buf.shape[-1]
    width = own.shape[-1] // tile
    pairs = [(q, c) for q in range(width) for c in range(2)]
    loads = [
        pltpu.make_async_copy(own.at[0, c, :, pl.ds(q * tile, tile)], hold.at[i], sem.at[i])
        for i, (q, c) in enumerate(pairs)
    ]
    stores = [pltpu.make_async_copy(hold.at[i], buf.at[i], sem.at[i]) for i in range(len(pairs))]
    for load in loads:
        load.start()
    for load, store in zip(loads, stores):
        load.wait()
        store.start()
    for store in stores:
        store.wait()


def route_kernel(start, ways, taken, sent, slots, tab, *refs):
    got = refs[2 : 2 + len(taken)]
    buf = refs[2 + len(taken)]
    outs = refs[4 + len(taken) : 4 + len(taken) + len(sent)]
    hold_in, hold_out, sem_in, sem_out = refs[-4:]

    def load_in(i):
        return pltpu.make_async_copy(got[i], hold_in.at[i], sem_in.at[i])

    def load_out(i, slot):
        return pltpu.make_async_copy(buf.at[slot], hold_out.at[i], sem_out.at[i])

    def store_in(i, slot):
        return pltpu.make_async_copy(hold_in.at[i], buf.at[slot], sem_in.at[i])

    def store_out(i):
        return pltpu.make_async_copy(hold_out.at[i], outs[i], sem_out.at[i])

    def pass_on(i, at):
        return pltpu.make_async_copy(hold_in.at[at], outs[i], sem_out.at[i])

    to = [tab[start + way] for way in taken]
    of = [tab[start + ways + way] for way in sent]
    for i, slot in enumerate(of):
        pl.when((slot >= 0) & (slot < slots))(lambda: load_out(i, slot).start())
    for i, slot in enumerate(to):
        pl.when(slot >= 0)(lambda: load_in(i).start())
    for i, slot in enumerate(of):
        @pl.when((slot >= 0) & (slot < slots))
        def _():
            load_out(i, slot).wait()
            store_out(i).start()
    for i, slot in enumerate(to):
        @pl.when(slot >= 0)
        def _():
            load_in(i).wait()
            store_in(i, slot).start()
    if taken:
        for i, slot in enumerate(of):
            pl.when(slot >= slots)(lambda: pass_on(i, slot - slots).start())
        for i, slot in enumerate(of):
            pl.when(slot >= slots)(lambda: pass_on(i, slot - slots).wait())
    for i, slot in enumerate(of):
        pl.when((slot >= 0) & (slot < slots))(lambda: store_out(i).wait())
    for i, slot in enumerate(to):
        pl.when(slot >= 0)(lambda: store_in(i, slot).wait())


def split(value):
    high = value.astype(jnp.bfloat16)
    return high, (value - high.astype(jnp.float32)).astype(jnp.bfloat16)


def multiply_kernel(start, first, tab, buf, *refs):
    if first:
        out, *scratch = refs
        acc_in = None
    else:
        acc_in, out, *scratch = refs
    acc, left, right, lcat, rcat, nt, sem_acc, sem_l, sem_r = scratch
    tile = buf.shape[-1]
    width = acc.shape[1]
    rows = min(256, tile)
    count = tab[start]

    def field(i, f):
        return tab[start + 1 + 9 * i + f]

    def acc_copies(ref, back):
        for c in range(2):
            for j in range(width):
                there, here = ref.at[0, c, :, pl.ds(j * tile, tile)], acc.at[c, j]
                pair = (here, there) if back else (there, here)
                yield pltpu.make_async_copy(*pair, sem_acc.at[c * width + j])

    def fetch_left(i, c):
        return pltpu.make_async_copy(buf.at[field(i, c)], left.at[c], sem_l.at[c])

    def fetch_right(i):
        return pltpu.make_async_copy(buf.at[field(i, 5)], right.at[lax.rem(i, 2)], sem_r.at[lax.rem(i, 2)])

    def fetch(i):
        fetch_right(i).start()

        @pl.when(field(i, 4) == 1)
        def _():
            fetch_left(i, 0).start()
            fetch_left(i, 1).start()

    @pl.when(count > 0)
    def _():
        fetch(0)

    if first:
        acc[...] = jnp.zeros_like(acc)
    else:
        for copy in acc_copies(acc_in, False):
            copy.start()
        for copy in acc_copies(acc_in, False):
            copy.wait()

    def op(i, carry):
        now = lax.rem(i, 2)
        fetch_right(i).wait()

        @pl.when(field(i, 4) == 1)
        def _():
            fetch_left(i, 0).wait()
            fetch_left(i, 1).wait()
            for c in range(2):
                @pl.when(field(i, 2 + c) == 1)
                def _():
                    left[c] = left[c].T

            def cut(r, carry):
                at = pl.ds(pl.multiple_of(r * rows, rows), rows)
                for c in range(2):
                    high, low = split(left[c, at, :])
                    lcat[c, at, 0:tile] = high
                    lcat[c, at, tile : 2 * tile] = high
                    lcat[c, at, 2 * tile :] = low
                return carry

            lax.fori_loop(0, tile // rows, cut, 0)

        @pl.when(i + 1 < count)
        def _():
            fetch(i + 1)

        j, c, turned = field(i, 7), field(i, 8), field(i, 6)

        def cut(r, carry):
            at = pl.ds(pl.multiple_of(r * rows, rows), rows)
            high, low = split(right[now, at, :])
            rcat[0, at, :] = high
            rcat[1, at, :] = low
            rcat[2, at, :] = high
            return carry

        lax.fori_loop(0, tile // rows, cut, 0)

        def product(turn):
            def part(r, carry):
                cl, half = r // (tile // rows), lax.rem(r, tile // rows)
                at = pl.ds(pl.multiple_of(half * rows, rows), rows)
                contract = ((1,), (1,)) if turn else ((1,), (0,))
                if turn:
                    total = sum(
                        lax.dot_general(
                            lcat[cl, at, m * tile : (m + 1) * tile],
                            rcat[m],
                            (contract, ((), ())),
                            preferred_element_type=jnp.float32,
                        )
                        for m in range(3)
                    )
                else:
                    total = jnp.dot(
                        lcat[cl, at, :],
                        rcat[...].reshape(3 * tile, tile),
                        preferred_element_type=jnp.float32,
                    )
                both = c * cl
                to = c + cl - 2 * both
                sign = (1 - 2 * both).astype(jnp.float32)
                acc[to, j, at, :] += sign * total
                return carry

            lax.fori_loop(0, 2 * (tile // rows), part, 0)

        @pl.when(turned == 0)
        def _():
            product(False)

        @pl.when(turned == 1)
        def _():
            product(True)

        return carry

    lax.fori_loop(0, count, op, 0)
    for copy in acc_copies(out, True):
        copy.start()
    for copy in acc_copies(out, True):
        copy.wait()


def local(src, rcv, recorded):
    perms, calls, longest, starts, table, slots, ways = plan(src, rcv)
    steps = len(perms)
    tile = recorded.shape[2]
    me = lax.axis_index("src") * rcv + lax.axis_index("rcv")
    tab = lax.dynamic_index_in_dim(jnp.asarray(table), me, 0, keepdims=False)
    chunk = jax.ShapeDtypeStruct((tile, tile), jnp.float32)
    buf_shape = jax.ShapeDtypeStruct((slots, tile, tile), jnp.float32)
    width = recorded.shape[3] // tile

    def call(kernel, ins, outs, scratch, aliases, cost, limit=None):
        return pl.pallas_call(
            kernel,
            out_shape=outs,
            grid_spec=pltpu.PrefetchScalarGridSpec(
                num_scalar_prefetch=1,
                grid=(),
                in_specs=[ANY] * len(ins),
                out_specs=[ANY] * len(outs),
                scratch_shapes=scratch,
            ),
            input_output_aliases=aliases,
            cost_estimate=pl.CostEstimate(flops=cost[0], bytes_accessed=cost[1], transcendentals=0),
            compiler_params=pltpu.CompilerParams(vmem_limit_bytes=limit),
        )(tab, *ins)

    size = tile * tile * 4
    (buf,) = call(
        first_kernel, [recorded], [buf_shape],
        [pltpu.VMEM((2 * width, tile, tile), jnp.float32), pltpu.SemaphoreType.DMA((2 * width,))],
        {}, (0, 4 * width * size), 48 << 20,
    )
    acc = None
    flight = {}
    for step in range(steps + 2):
        got = flight.pop(step - 2, {})
        taken = sorted(got)
        sent = [way for way in range(ways) if step < steps and perms[step][way]]
        ins = [buf, recorded if acc is None else acc] + [got[way] for way in taken]
        outs = [buf_shape, jax.ShapeDtypeStruct(recorded.shape, jnp.float32)] + [chunk] * len(sent)
        aliases = {1: 0} if acc is None else {1: 0, 2: 1}
        if acc is None:
            ins.pop(1)
            outs.pop(1)
            kernel = functools.partial(first_route, starts["route", step], ways, taken, sent, slots)
        else:
            kernel = functools.partial(route_kernel, starts["route", step], ways, taken, sent, slots)
        done = call(
            kernel,
            ins,
            outs,
            [
                pltpu.VMEM((max(len(taken), 1), tile, tile), jnp.float32),
                pltpu.VMEM((max(len(sent), 1), tile, tile), jnp.float32),
                pltpu.SemaphoreType.DMA((max(len(taken), 1),)),
                pltpu.SemaphoreType.DMA((max(len(sent), 1),)),
            ],
            aliases,
            (0, 2 * (len(taken) + len(sent)) * size),
            24 << 20,
        )
        if acc is None:
            buf, *out = done
        else:
            buf, acc, *out = done
        flight[step] = {
            way: lax.ppermute(value, AXES, perms[step][way]) for way, value in zip(sent, out)
        }
        if step in calls:
            ops = longest[calls.index(step)]
            first = acc is None
            scratch = [
                pltpu.VMEM((2, width, tile, tile), jnp.float32),
                pltpu.VMEM((2, tile, tile), jnp.float32),
                pltpu.VMEM((2, tile, tile), jnp.float32),
                pltpu.VMEM((2, tile, 3 * tile), jnp.bfloat16),
                pltpu.VMEM((3, tile, tile), jnp.bfloat16),
                pltpu.SMEM((1,), jnp.int32),
                pltpu.SemaphoreType.DMA((2 * width,)),
                pltpu.SemaphoreType.DMA((2,)),
                pltpu.SemaphoreType.DMA((2,)),
            ]
            (acc,) = call(
                functools.partial(multiply_kernel, starts["ops", step], first),
                [buf] if first else [buf, acc],
                [jax.ShapeDtypeStruct(recorded.shape, jnp.float32)],
                scratch,
                {} if first else {2: 0},
                (ops * 12 * tile**3, ops * 3 * size + 4 * width * size),
                48 << 20,
            )
    return acc


def first_route(start, ways, taken, sent, slots, tab, *refs):
    buf, rest = refs[0], refs[1:]
    got, rest = rest[: len(taken)], rest[len(taken) :]
    route_kernel(start, ways, taken, sent, slots, tab, buf, None, *got, rest[0], None, *rest[1:])


def solution(mesh):
    src, rcv = mesh.shape["src"], mesh.shape["rcv"]
    return jax.shard_map(
        functools.partial(local, src, rcv),
        mesh=mesh,
        in_specs=(P("freq", None, "src", "rcv"),),
        out_specs=P("freq", None, "src", "rcv"),
        check_vma=False,
    )
```

```python
import functools
import random

import jax
import jax.numpy as jnp
import numpy as np
from jax import lax
from jax.experimental import pallas as pl
from jax.experimental.pallas import tpu as pltpu
from jax.sharding import PartitionSpec as P

AXES = ("src", "rcv")
FIELDS = 6
CAP = 6


def split_axis(n):
    return (n,) if n <= 4 else (4, n // 4)


class Grid:
    def __init__(self, src, rcv):
        self.src, self.rcv, self.width = src, rcv, src // rcv
        dims = split_axis(src) + split_axis(rcv)
        self.count = src * rcv
        place = np.array(np.unravel_index(np.arange(self.count), dims)).T
        self.dist = np.abs(place[:, None] - place[None]).sum(-1)
        self.ways = []
        for axis, size in enumerate(dims):
            for sign in (1, -1) if size > 2 else (0,):
                pairs = []
                for u in range(self.count):
                    to = place[u].copy()
                    to[axis] = 1 - to[axis] if sign == 0 else to[axis] + sign
                    if 0 <= to[axis] < size:
                        pairs.append((u, int(np.ravel_multi_index(tuple(to), dims))))
                if pairs:
                    self.ways.append(pairs)
        self.tiles = [(p, q) for p in range(src) for q in range(p, src)]
        self.number = {}
        for i, (p, q) in enumerate(self.tiles):
            self.number[p, q] = self.number[q, p] = i

    def columns(self, x):
        return range(x * self.width, (x + 1) * self.width)


def plan_moves(grid, seed):
    rnd = random.Random(seed)
    items, n = len(grid.tiles), grid.count
    has = np.full((n, items), 10**6)
    need = np.zeros((n, items), bool)
    row = np.zeros((n, items), bool)
    flip = np.zeros((n, items), bool)
    for d in range(n):
        s, x = divmod(d, grid.rcv)
        for q in range(grid.src):
            need[d, grid.number[s, q]] = True
            row[d, grid.number[s, q]] = True
            for j in grid.columns(x):
                need[d, grid.number[q, j]] = True
        for q in grid.columns(x):
            has[d, grid.number[s, q]] = 0
            flip[d, grid.number[s, q]] = s > q
    links = [(way, u, v) for way, pairs in enumerate(grid.ways) for u, v in pairs]
    degree = np.zeros(n)
    for _, _, v in links:
        degree[v] += 1
    near = np.stack([grid.dist[has[:, i] == 0].min(0) for i in range(items)])
    moves, step = [], 0
    while True:
        missing = need & (has > 10**5)
        if not missing.any():
            return moves, has, flip
        load = missing.sum(1) / degree
        weight = missing.sum(1) / np.maximum(need.sum(1), 1)
        rnd.shuffle(links)
        links.sort(key=lambda link: -load[link[2]])
        open_ = has > 10**5
        into = [[] for _ in range(n)]
        for _, u, v in links:
            into[v].append(u)
        ready = has <= step
        now = []
        for way, u, v in links:
            cand = np.nonzero(ready[u] & open_[v])[0]
            if not len(cand):
                continue
            helped = (missing[:, cand].T & (grid.dist[v][None] < near[cand])).astype(float)
            helped[:, v] = 0
            value = 3.0 * missing[v, cand] + helped @ weight
            useful = value > 0
            if not useful.any():
                continue
            others = sum(ready[w, cand].astype(float) for w in into[v])
            value = value + 0.5 * np.array([rnd.random() for _ in cand]) - 0.7 * (others - 1)
            value = value + 3.0 * (row[v, cand] & missing[v, cand])
            value[~useful] = -100
            item = int(cand[np.argmax(value)])
            open_[v, item] = False
            missing[v, item] = False
            near[item] = np.minimum(near[item], grid.dist[v])
            now.append((way, u, v, item))
        for _, u, v, item in now:
            has[v, item] = step + 2
            flip[v, item] = flip[u, item]
        moves.append(now)
        step += 1


def plan_products(grid, moves, has, flip):
    steps, n = len(moves), grid.count
    calls = [*range(3, steps + 2)]
    lists = [[[] for _ in range(n)] for _ in calls]
    for d in range(n):
        s, x = divmod(d, grid.rcv)
        todo = []
        for k in range(grid.src):
            left = grid.number[s, k]
            for j, q in enumerate(grid.columns(x)):
                right = grid.number[k, q]
                todo.append((max(has[d, left], has[d, right]), k, j, left, right, q))
        todo.sort()
        for at, step in enumerate(calls):
            fit = [one for one in todo if one[0] <= step]
            if step < steps + 1:
                alike = {j: sum(one[2] == j for one in fit) for j in range(grid.width)}
                fit.sort(key=lambda one: (-alike[one[2]], one[2], one[0]))
                fit = fit[:CAP]
            fit.sort(key=lambda one: (one[2], one[0]))
            todo = [one for one in todo if one not in fit]
            lists[at][d] = [one[1:] for one in fit]
        assert not todo
    return calls, lists


@functools.lru_cache(None)
def plan(src, rcv):
    grid = Grid(src, rcv)
    best = None
    for seed in range(240 if grid.count <= 16 else 1):
        got = plan_moves(grid, seed)
        calls, work = plan_products(grid, *got)
        late = [max(len(per) for per in lists) for lists in work[-3:]]
        cost = 46 * len(got[0]) + 4 * (late[2] + max(late[1] - 5, 0) + max(late[0] - 5, 0))
        if best is None or cost < best[0]:
            best = cost, got, calls, work
    (moves, has, flip), calls, work = best[1:]
    n, ways, steps = grid.count, len(grid.ways), len(moves)
    slot = np.full((n, len(grid.tiles)), -1)
    used = np.zeros(n, int)
    for d in range(n):
        s, x = divmod(d, rcv)
        for q in grid.columns(x):
            slot[d, grid.number[s, q]] = used[d]
            used[d] += 1
    keep = np.zeros((n, len(grid.tiles)), bool)
    for step, now in enumerate(moves):
        for way, u, v, item in now:
            keep[u, item] |= has[u, item] < step
    send = np.full((steps + 2, ways, n), -1)
    take = np.full((steps + 2, ways, n), -1)
    turn = np.zeros((steps + 2, ways, n), int)
    use = np.zeros((n, len(grid.tiles)), bool)
    rows = np.zeros((n, len(grid.tiles)), int)
    for d in range(n):
        s, x = divmod(d, rcv)
        for i in range(len(grid.tiles)):
            p, q = grid.tiles[i]
            rows[d, i] = s if s in (p, q) else p if q in grid.columns(x) else q
            use[d, i] = s in (p, q) or p in grid.columns(x) or q in grid.columns(x)
    place = slot.copy()
    other = np.full((n, len(grid.tiles)), -1)
    placed = used.copy()
    both = np.zeros((n, len(grid.tiles)), bool)
    for d in range(n):
        for i in range(len(grid.tiles)):
            p, q = grid.tiles[i]
            s, at = d // rcv, grid.columns(d % rcv)
            both[d, i] = p != q and (p in at and q in at or s in (p, q) and s in at)
            if place[d, i] >= 0 and both[d, i]:
                other[d, i] = placed[d]
                placed[d] += 1
    perms = [[[] for _ in range(ways)] for _ in range(steps)]
    for step, now in enumerate(moves):
        for way, u, v, item in now:
            if keep[v, item]:
                slot[v, item] = used[v]
                used[v] += 1
            take[step + 2, way, v] = item
            if use[v, item]:
                place[v, item] = placed[v]
                placed[v] += 1
                if both[v, item]:
                    other[v, item] = placed[v]
                    placed[v] += 1
                p, q = grid.tiles[item]
                turn[step + 2, way, v] = int(p != q and (rows[v, item] == q) != flip[v, item])
            perms[step][way].append((u, v))
    for step, now in enumerate(moves):
        taken = [way for way in range(ways) if step >= 2 and perms[step - 2][way]]
        for way, u, v, item in now:
            new = [i for i, w in enumerate(taken) if take[step, w, u] == item]
            send[step, way, u] = used.max() + new[0] if new else slot[u, item]
    kept = np.full((steps + 2, ways, n), -1)
    store = np.full((steps + 2, ways, n), -1)
    again = np.full((steps + 2, ways, n), -1)
    for step, now in enumerate(moves):
        for way, u, v, item in now:
            kept[step + 2, way, v] = slot[v, item]
            store[step + 2, way, v] = place[v, item]
            again[step + 2, way, v] = other[v, item]
    lists = [[[] for _ in range(n)] for _ in calls]
    fresh = [set() for _ in range(n)]
    for at, per in enumerate(work):
        for d in range(n):
            s = d // rcv
            for i, (k, j, left, right, q) in enumerate(per[d]):
                begin = i == 0 or per[d][i - 1][1] != j
                end = i + 1 == len(per[d]) or per[d][i + 1][1] != j
                over = other[d, right] if k != q and rows[d, right] != k else place[d, right]
                assert over >= 0
                mode = 0 if not begin else 1 if j in fresh[d] else 2
                fresh[d].add(j)
                group = len({one[1] for one in per[d][: i + 1]}) - 1
                lists[at][d].append((place[d, left], over, j, mode, int(end), group))
    longest = [max(len(one) for one in per) for per in lists]
    table = []
    starts = {"own": 0}
    for q in range(grid.width):
        table.append(np.array([other[d, grid.number[d // rcv, d % rcv * grid.width + q]] for d in range(n)]))
    for step in range(steps + 2):
        starts["route", step] = len(table)
        for what in (take, send, kept, store, turn, again):
            for way in range(ways):
                table.append(what[step, way])
    for at, step in enumerate(calls):
        starts["ops", step] = len(table)
        table.append(np.array([len(lists[at][d]) for d in range(n)]))
        table.append(np.array([lists[at][d][-1][5] + 1 if lists[at][d] else 0 for d in range(n)]))
        for i in range(longest[at]):
            for f in range(FIELDS):
                table.append(np.array([lists[at][d][i][f] if i < len(lists[at][d]) else 0 for d in range(n)]))
    return perms, calls, longest, starts, np.array(table, np.int32).T.copy(), int(used.max()), int(placed.max()), ways


ANY = pl.BlockSpec(memory_space=pl.ANY)


def split(value):
    high = value.astype(jnp.bfloat16)
    return high, (value - high.astype(jnp.float32)).astype(jnp.bfloat16)


def cut(ref, at, out, to, turn):
    tile = ref.shape[-1]
    rows = min(128, tile)
    count = tile // rows

    def block(r):
        return pl.ds(pl.multiple_of(r * rows, rows), rows)

    def straight(i, carry):
        c, r = i // count, lax.rem(i, count)
        out[to, c, 0, block(r), :], out[to, c, 1, block(r), :] = split(ref[at, c, block(r), :])
        return carry

    def across(i, carry):
        c, r = i // count, lax.rem(i, count)
        out[to, c, 0, block(r), :], out[to, c, 1, block(r), :] = split(ref[at, c, :, block(r)].T)
        return carry

    @pl.when(turn == 0)
    def _():
        lax.fori_loop(0, 2 * count, straight, 0)

    @pl.when(turn != 0)
    def _():
        lax.fori_loop(0, 2 * count, across, 0)


def first_kernel(tab, own, buf, cuts, hold, ready, sem, sem_cut):
    tile = buf.shape[-1]
    width = own.shape[-1] // tile

    def load(i):
        for c in range(2):
            yield pltpu.make_async_copy(own.at[0, c, :, pl.ds(i * tile, tile)], hold.at[i, c], sem.at[i, c])

    def store(i):
        return pltpu.make_async_copy(hold.at[i], buf.at[i], sem.at[i, 0])

    def write(i):
        return pltpu.make_async_copy(ready.at[i], cuts.at[i], sem_cut.at[i])

    def again(i):
        return pltpu.make_async_copy(ready.at[width + i], cuts.at[tab[i]], sem_cut.at[width + i])

    for i in range(width):
        for copy in load(i):
            copy.start()
    for i in range(width):
        for copy in load(i):
            copy.wait()
        store(i).start()

    def part(i, carry):
        cut(hold, i, ready, i, 0)
        write(i).start()

        @pl.when(tab[i] >= 0)
        def _():
            cut(hold, i, ready, width + i, 1)
            again(i).start()

        return carry

    lax.fori_loop(0, width, part, 0)
    for i in range(width):
        store(i).wait()
        write(i).wait()
        pl.when(tab[i] >= 0)(lambda: again(i).wait())


def route_kernel(start, ways, taken, sent, slots, tab, *refs):
    got = refs[3 : 3 + len(taken)]
    buf, cuts = refs[3 + len(taken) : 5 + len(taken)]
    outs = refs[6 + len(taken) : 6 + len(taken) + len(sent)]
    hold_in, hold_out, ready, sem_in, sem_out, sem_cut = refs[-6:]

    def load_in(i):
        return pltpu.make_async_copy(got[i], hold_in.at[i], sem_in.at[i])

    def load_out(i, slot):
        return pltpu.make_async_copy(buf.at[slot], hold_out.at[i], sem_out.at[i])

    def store_in(i, slot):
        return pltpu.make_async_copy(hold_in.at[i], buf.at[slot], sem_in.at[i])

    def store_out(i):
        return pltpu.make_async_copy(hold_out.at[i], outs[i], sem_out.at[i])

    def pass_on(i, at):
        return pltpu.make_async_copy(hold_in.at[at], outs[i], sem_out.at[i])

    def write(i, slot):
        return pltpu.make_async_copy(ready.at[i], cuts.at[slot], sem_cut.at[i])

    def again(i):
        at = len(taken) + i
        return pltpu.make_async_copy(ready.at[at], cuts.at[entry(5, taken[i])], sem_cut.at[at])

    def entry(kind, way):
        return tab[start + kind * ways + way]

    to = [entry(0, way) for way in taken]
    of = [entry(1, way) for way in sent]
    keep = [entry(2, way) for way in taken]
    place = [entry(3, way) for way in taken]
    for i, slot in enumerate(of):
        pl.when((slot >= 0) & (slot < slots))(lambda: load_out(i, slot).start())
    for i, slot in enumerate(to):
        pl.when(slot >= 0)(lambda: load_in(i).start())
    for i, slot in enumerate(of):
        @pl.when((slot >= 0) & (slot < slots))
        def _():
            load_out(i, slot).wait()
            store_out(i).start()
    for i, slot in enumerate(to):
        pl.when(slot >= 0)(lambda: load_in(i).wait())
        pl.when(keep[i] >= 0)(lambda: store_in(i, keep[i]).start())
    if taken:
        for i, slot in enumerate(of):
            pl.when(slot >= slots)(lambda: pass_on(i, slot - slots).start())
        for i, way in enumerate(taken):
            @pl.when(place[i] >= 0)
            def _():
                cut(hold_in, i, ready, i, entry(4, way))
                write(i, place[i]).start()

                @pl.when(entry(5, way) >= 0)
                def _():
                    cut(hold_in, i, ready, len(taken) + i, 1 - entry(4, way))
                    again(i).start()
        for i, slot in enumerate(of):
            pl.when(slot >= slots)(lambda: pass_on(i, slot - slots).wait())
    for i, slot in enumerate(of):
        pl.when((slot >= 0) & (slot < slots))(lambda: store_out(i).wait())
    for i in range(len(taken)):
        pl.when(keep[i] >= 0)(lambda: store_in(i, keep[i]).wait())
        pl.when(place[i] >= 0)(lambda: write(i, place[i]).wait())
        pl.when(entry(5, taken[i]) >= 0)(lambda: again(i).wait())


def multiply_kernel(start, first, tab, cuts, *refs):
    if first:
        out, *scratch = refs
        before = None
    else:
        before, out, *scratch = refs
    total, left, right, sem_get, sem_put, sem_l, sem_r = scratch
    tile = cuts.shape[-1]
    count = tab[start]

    def field(i, f):
        return tab[start + 2 + FIELDS * i + f]

    def columns(ref, c, j):
        return ref.at[0, c, :, pl.ds(pl.multiple_of(j * tile, tile), tile)]

    def fetch(i):
        now = lax.rem(i, 2)
        yield pltpu.make_async_copy(cuts.at[field(i, 0)], left.at[now], sem_l.at[now])
        yield pltpu.make_async_copy(cuts.at[field(i, 1)], right.at[now], sem_r.at[now])

    def get(i):
        at = lax.rem(field(i, 5), 2)
        for c in range(2):
            yield pltpu.make_async_copy(columns(before, c, field(i, 2)), total.at[at, c], sem_get.at[2 * at + c])

    def put(group, j):
        at = lax.rem(group, 2)
        for c in range(2):
            yield pltpu.make_async_copy(total.at[at, c], columns(out, c, j), sem_put.at[2 * at + c])

    def begin(i):
        for copy in fetch(i):
            copy.start()

        @pl.when((field(i, 3) > 0) & (field(i, 5) > 1))
        def _():
            for copy in put(field(i, 5), 0):
                copy.wait()

        if not first:
            @pl.when(field(i, 3) == 1)
            def _():
                for copy in get(i):
                    copy.start()

    @pl.when(count > 0)
    def _():
        begin(0)

    def op(i, carry):
        now = lax.rem(i, 2)
        at = lax.rem(field(i, 5), 2)
        if not first:
            @pl.when(field(i, 3) == 1)
            def _():
                for copy in get(i):
                    copy.wait()

        @pl.when(field(i, 3) == 2)
        def _():
            total[at] = jnp.zeros((2, tile, tile), jnp.float32)

        for copy in fetch(i):
            copy.wait()

        @pl.when(i + 1 < count)
        def _():
            begin(i + 1)

        def product(step, carry):
            cl, c = step // 2, lax.rem(step, 2)
            to = cl + c - 2 * cl * c
            sign = (1 - 2 * cl * c).astype(jnp.float32)
            one = jnp.concatenate([left[now, cl, 0], left[now, cl, 0], left[now, cl, 1]], axis=1)
            two = jnp.concatenate([right[now, c, 0], right[now, c, 1], right[now, c, 0]], axis=0)
            total[at, to] += sign * jnp.dot(one, two, preferred_element_type=jnp.float32)
            return carry

        lax.fori_loop(0, 4, product, 0)

        @pl.when(field(i, 4) == 1)
        def _():
            for copy in put(field(i, 5), field(i, 2)):
                copy.start()

        return carry

    lax.fori_loop(0, count, op, 0)
    for back in (2, 1):
        @pl.when(tab[start + 1] >= back)
        def _():
            for copy in put(tab[start + 1] - back, 0):
                copy.wait()


def local(src, rcv, recorded):
    perms, calls, longest, starts, table, slots, places, ways = plan(src, rcv)
    steps = len(perms)
    tile = recorded.shape[2]
    me = lax.axis_index("src") * rcv + lax.axis_index("rcv")
    tab = lax.dynamic_index_in_dim(jnp.asarray(table), me, 0, keepdims=False)
    chunk = jax.ShapeDtypeStruct((2, tile, tile), jnp.float32)
    buf_shape = jax.ShapeDtypeStruct((slots, 2, tile, tile), jnp.float32)
    cut_shape = jax.ShapeDtypeStruct((places, 2, 2, tile, tile), jnp.bfloat16)
    acc_shape = jax.ShapeDtypeStruct(recorded.shape, jnp.float32)
    width = recorded.shape[3] // tile

    def call(kernel, ins, outs, scratch, aliases, cost, limit=None):
        return pl.pallas_call(
            kernel,
            out_shape=outs,
            grid_spec=pltpu.PrefetchScalarGridSpec(
                num_scalar_prefetch=1,
                grid=(),
                in_specs=[ANY] * len(ins),
                out_specs=[ANY] * len(outs),
                scratch_shapes=scratch,
            ),
            input_output_aliases=aliases,
            cost_estimate=pl.CostEstimate(flops=cost[0], bytes_accessed=cost[1], transcendentals=0),
            compiler_params=pltpu.CompilerParams(vmem_limit_bytes=limit),
        )(tab, *ins)

    size = tile * tile * 8
    buf, cuts = call(
        first_kernel,
        [recorded],
        [buf_shape, cut_shape],
        [
            pltpu.VMEM((width, 2, tile, tile), jnp.float32),
            pltpu.VMEM((2 * width, 2, 2, tile, tile), jnp.bfloat16),
            pltpu.SemaphoreType.DMA((width, 2)),
            pltpu.SemaphoreType.DMA((2 * width,)),
        ],
        {},
        (0, 3 * width * size),
        48 << 20,
    )
    acc = None
    flight = {}
    for step in range(steps + 2):
        got = flight.pop(step - 2, {})
        taken = sorted(got)
        sent = [way for way in range(ways) if step < steps and perms[step][way]]
        state = [buf, cuts] if acc is None else [buf, cuts, acc]
        m = len(state)
        kernel = functools.partial(
            route_kernel if m == 3 else first_route, starts["route", step], ways, taken, sent, slots
        )
        done = call(
            kernel,
            state + [got[way] for way in taken],
            [buf_shape, cut_shape, acc_shape][:m] + [chunk] * len(sent),
            [
                pltpu.VMEM((max(len(taken), 1), 2, tile, tile), jnp.float32),
                pltpu.VMEM((max(len(sent), 1), 2, tile, tile), jnp.float32),
                pltpu.VMEM((max(2 * len(taken), 1), 2, 2, tile, tile), jnp.bfloat16),
                pltpu.SemaphoreType.DMA((max(len(taken), 1),)),
                pltpu.SemaphoreType.DMA((max(len(sent), 1),)),
                pltpu.SemaphoreType.DMA((max(2 * len(taken), 1),)),
            ],
            {1 + i: i for i in range(m)},
            (0, (3 * len(taken) + 2 * len(sent)) * size),
            50 << 20,
        )
        buf, cuts = done[:2]
        if m == 3:
            acc = done[2]
        flight[step] = {
            way: lax.ppermute(value, AXES, perms[step][way]) for way, value in zip(sent, done[m:])
        }
        if step in calls and longest[calls.index(step)]:
            ops = longest[calls.index(step)]
            first = acc is None
            (acc,) = call(
                functools.partial(multiply_kernel, starts["ops", step], first),
                [cuts] if first else [cuts, acc],
                [acc_shape],
                [
                    pltpu.VMEM((2, 2, tile, tile), jnp.float32),
                    pltpu.VMEM((2, 2, 2, tile, tile), jnp.bfloat16),
                    pltpu.VMEM((2, 2, 2, tile, tile), jnp.bfloat16),
                    pltpu.SemaphoreType.DMA((4,)),
                    pltpu.SemaphoreType.DMA((4,)),
                    pltpu.SemaphoreType.DMA((2,)),
                    pltpu.SemaphoreType.DMA((2,)),
                ],
                {} if first else {2: 0},
                (ops * 24 * tile**3, ops * 3 * size),
                32 << 20,
            )
    return acc


def first_route(start, ways, taken, sent, slots, tab, *refs):
    n = 2 + len(taken)
    route_kernel(start, ways, taken, sent, slots, tab, *refs[:2], None, *refs[2 : n + 2], None, *refs[n + 2 :])


def solution(mesh):
    src, rcv = mesh.shape["src"], mesh.shape["rcv"]
    return jax.shard_map(
        functools.partial(local, src, rcv),
        mesh=mesh,
        in_specs=(P("freq", None, "src", "rcv"),),
        out_specs=P("freq", None, "src", "rcv"),
        check_vma=False,
    )
```

```python
import functools
import random

import jax
import jax.numpy as jnp
import numpy as np
from jax import lax
from jax.experimental import pallas as pl
from jax.experimental.pallas import tpu as pltpu
from jax.sharding import PartitionSpec as P

AXES = ("src", "rcv")
FIELDS = 6
CAP = 6


def split_axis(n):
    return (n,) if n <= 4 else (4, n // 4)


class Grid:
    def __init__(self, src, rcv):
        self.src, self.rcv, self.width = src, rcv, src // rcv
        dims = split_axis(src) + split_axis(rcv)
        self.count = src * rcv
        place = np.array(np.unravel_index(np.arange(self.count), dims)).T
        self.dist = np.abs(place[:, None] - place[None]).sum(-1)
        self.ways = []
        for axis, size in enumerate(dims):
            for sign in (1, -1) if size > 2 else (0,):
                pairs = []
                for u in range(self.count):
                    to = place[u].copy()
                    to[axis] = 1 - to[axis] if sign == 0 else to[axis] + sign
                    if 0 <= to[axis] < size:
                        pairs.append((u, int(np.ravel_multi_index(tuple(to), dims))))
                if pairs:
                    self.ways.append(pairs)
        self.tiles = [(p, q) for p in range(src) for q in range(p, src)]
        self.number = {}
        for i, (p, q) in enumerate(self.tiles):
            self.number[p, q] = self.number[q, p] = i

    def columns(self, x):
        return range(x * self.width, (x + 1) * self.width)


def plan_moves(grid, seed):
    rnd = random.Random(seed)
    items, n = len(grid.tiles), grid.count
    has = np.full((n, items), 10**6)
    need = np.zeros((n, items), bool)
    row = np.zeros((n, items), bool)
    flip = np.zeros((n, items), bool)
    for d in range(n):
        s, x = divmod(d, grid.rcv)
        for q in range(grid.src):
            need[d, grid.number[s, q]] = True
            row[d, grid.number[s, q]] = True
            for j in grid.columns(x):
                need[d, grid.number[q, j]] = True
        for q in grid.columns(x):
            has[d, grid.number[s, q]] = 0
            flip[d, grid.number[s, q]] = s > q
    links = [(way, u, v) for way, pairs in enumerate(grid.ways) for u, v in pairs]
    degree = np.zeros(n)
    for _, _, v in links:
        degree[v] += 1
    near = np.stack([grid.dist[has[:, i] == 0].min(0) for i in range(items)])
    moves, step = [], 0
    while True:
        missing = need & (has > 10**5)
        if not missing.any():
            return moves, has, flip
        load = missing.sum(1) / degree
        weight = missing.sum(1) / np.maximum(need.sum(1), 1)
        rnd.shuffle(links)
        links.sort(key=lambda link: -load[link[2]])
        open_ = has > 10**5
        into = [[] for _ in range(n)]
        for _, u, v in links:
            into[v].append(u)
        ready = has <= step
        now = []
        for way, u, v in links:
            cand = np.nonzero(ready[u] & open_[v])[0]
            if not len(cand):
                continue
            helped = (missing[:, cand].T & (grid.dist[v][None] < near[cand])).astype(float)
            helped[:, v] = 0
            value = 3.0 * missing[v, cand] + helped @ weight
            useful = value > 0
            if not useful.any():
                continue
            others = sum(ready[w, cand].astype(float) for w in into[v])
            value = value + 0.5 * np.array([rnd.random() for _ in cand]) - 0.7 * (others - 1)
            value = value + 3.0 * (row[v, cand] & missing[v, cand])
            value[~useful] = -100
            item = int(cand[np.argmax(value)])
            open_[v, item] = False
            missing[v, item] = False
            near[item] = np.minimum(near[item], grid.dist[v])
            now.append((way, u, v, item))
        for _, u, v, item in now:
            has[v, item] = step + 2
            flip[v, item] = flip[u, item]
        moves.append(now)
        step += 1


def plan_products(grid, moves, has, flip):
    steps, n = len(moves), grid.count
    calls = [*range(3, steps + 2)]
    lists = [[[] for _ in range(n)] for _ in calls]
    for d in range(n):
        s, x = divmod(d, grid.rcv)
        todo = []
        for k in range(grid.src):
            left = grid.number[s, k]
            for j, q in enumerate(grid.columns(x)):
                right = grid.number[k, q]
                todo.append((max(has[d, left], has[d, right]), k, j, left, right, q))
        todo.sort()
        for at, step in enumerate(calls):
            fit = [one for one in todo if one[0] <= step]
            if step < steps + 1:
                alike = {j: sum(one[2] == j for one in fit) for j in range(grid.width)}
                fit.sort(key=lambda one: (-alike[one[2]], one[2], one[0]))
                fit = fit[:CAP]
            fit.sort(key=lambda one: (one[2], one[0]))
            todo = [one for one in todo if one not in fit]
            lists[at][d] = [one[1:] for one in fit]
        assert not todo
    return calls, lists


@functools.lru_cache(None)
def plan(src, rcv):
    grid = Grid(src, rcv)
    best = None
    for seed in range(240 if grid.count <= 16 else 1):
        got = plan_moves(grid, seed)
        calls, work = plan_products(grid, *got)
        late = [max(len(per) for per in lists) for lists in work[-3:]]
        cost = 46 * len(got[0]) + 4 * (late[2] + max(late[1] - 5, 0) + max(late[0] - 5, 0))
        if best is None or cost < best[0]:
            best = cost, got, calls, work
    (moves, has, flip), calls, work = best[1:]
    n, ways, steps = grid.count, len(grid.ways), len(moves)
    slot = np.full((n, len(grid.tiles)), -1)
    used = np.zeros(n, int)
    for d in range(n):
        s, x = divmod(d, rcv)
        for q in grid.columns(x):
            slot[d, grid.number[s, q]] = used[d]
            used[d] += 1
    keep = np.zeros((n, len(grid.tiles)), bool)
    for step, now in enumerate(moves):
        for way, u, v, item in now:
            keep[u, item] |= has[u, item] < step
    send = np.full((steps + 2, ways, n), -1)
    take = np.full((steps + 2, ways, n), -1)
    turn = np.zeros((steps + 2, ways, n), int)
    use = np.zeros((n, len(grid.tiles)), bool)
    rows = np.zeros((n, len(grid.tiles)), int)
    for d in range(n):
        s, x = divmod(d, rcv)
        for i in range(len(grid.tiles)):
            p, q = grid.tiles[i]
            rows[d, i] = s if s in (p, q) else p if q in grid.columns(x) else q
            use[d, i] = s in (p, q) or p in grid.columns(x) or q in grid.columns(x)
    place = slot.copy()
    other = np.full((n, len(grid.tiles)), -1)
    placed = used.copy()
    both = np.zeros((n, len(grid.tiles)), bool)
    for d in range(n):
        for i in range(len(grid.tiles)):
            p, q = grid.tiles[i]
            s, at = d // rcv, grid.columns(d % rcv)
            both[d, i] = p != q and (p in at and q in at or s in (p, q) and s in at)
            if place[d, i] >= 0 and both[d, i]:
                other[d, i] = placed[d]
                placed[d] += 1
    perms = [[[] for _ in range(ways)] for _ in range(steps)]
    for step, now in enumerate(moves):
        for way, u, v, item in now:
            if keep[v, item]:
                slot[v, item] = used[v]
                used[v] += 1
            take[step + 2, way, v] = item
            if use[v, item]:
                place[v, item] = placed[v]
                placed[v] += 1
                if both[v, item]:
                    other[v, item] = placed[v]
                    placed[v] += 1
                p, q = grid.tiles[item]
                turn[step + 2, way, v] = int(p != q and (rows[v, item] == q) != flip[v, item])
            perms[step][way].append((u, v))
    for step, now in enumerate(moves):
        taken = [way for way in range(ways) if step >= 2 and perms[step - 2][way]]
        for way, u, v, item in now:
            new = [i for i, w in enumerate(taken) if take[step, w, u] == item]
            send[step, way, u] = used.max() + new[0] if new else slot[u, item]
    kept = np.full((steps + 2, ways, n), -1)
    store = np.full((steps + 2, ways, n), -1)
    again = np.full((steps + 2, ways, n), -1)
    for step, now in enumerate(moves):
        for way, u, v, item in now:
            kept[step + 2, way, v] = slot[v, item]
            store[step + 2, way, v] = place[v, item]
            again[step + 2, way, v] = other[v, item]
    lists = [[[] for _ in range(n)] for _ in calls]
    fresh = [set() for _ in range(n)]
    for at, per in enumerate(work):
        for d in range(n):
            s = d // rcv
            for i, (k, j, left, right, q) in enumerate(per[d]):
                begin = i == 0 or per[d][i - 1][1] != j
                end = i + 1 == len(per[d]) or per[d][i + 1][1] != j
                over = other[d, right] if k != q and rows[d, right] != k else place[d, right]
                assert over >= 0
                mode = 0 if not begin else 1 if j in fresh[d] else 2
                fresh[d].add(j)
                group = len({one[1] for one in per[d][: i + 1]}) - 1
                lists[at][d].append((place[d, left], over, j, mode, int(end), group))
    longest = [max(len(one) for one in per) for per in lists]
    table = []
    starts = {"own": 0}
    for q in range(grid.width):
        table.append(np.array([other[d, grid.number[d // rcv, d % rcv * grid.width + q]] for d in range(n)]))
    for step in range(steps + 2):
        starts["route", step] = len(table)
        for what in (take, send, kept, store, turn, again):
            for way in range(ways):
                table.append(what[step, way])
    for at, step in enumerate(calls):
        starts["ops", step] = len(table)
        table.append(np.array([len(lists[at][d]) for d in range(n)]))
        table.append(np.array([lists[at][d][-1][5] + 1 if lists[at][d] else 0 for d in range(n)]))
        for i in range(longest[at]):
            for f in range(FIELDS):
                table.append(np.array([lists[at][d][i][f] if i < len(lists[at][d]) else 0 for d in range(n)]))
    return perms, calls, longest, starts, np.array(table, np.int32).T.copy(), int(used.max()), int(placed.max()), ways


ANY = pl.BlockSpec(memory_space=pl.ANY)


def split(value):
    high = value.astype(jnp.bfloat16)
    return high, (value - high.astype(jnp.float32)).astype(jnp.bfloat16)


def cut(ref, at, out, to, turn):
    tile = ref.shape[-1]
    rows = min(128, tile)
    count = tile // rows

    def block(r):
        return pl.ds(pl.multiple_of(r * rows, rows), rows)

    def straight(i, carry):
        c, r = i // count, lax.rem(i, count)
        out[to, c, 0, block(r), :], out[to, c, 1, block(r), :] = split(ref[at, c, block(r), :])
        return carry

    def across(i, carry):
        c, r = i // count, lax.rem(i, count)
        out[to, c, 0, block(r), :], out[to, c, 1, block(r), :] = split(ref[at, c, :, block(r)].T)
        return carry

    @pl.when(turn == 0)
    def _():
        lax.fori_loop(0, 2 * count, straight, 0)

    @pl.when(turn != 0)
    def _():
        lax.fori_loop(0, 2 * count, across, 0)


def first_kernel(tab, own, buf, cuts, hold, ready, sem, sem_cut):
    tile = buf.shape[-1]
    width = own.shape[-1] // tile

    def load(i):
        for c in range(2):
            yield pltpu.make_async_copy(own.at[0, c, :, pl.ds(i * tile, tile)], hold.at[i, c], sem.at[i, c])

    def store(i):
        return pltpu.make_async_copy(hold.at[i], buf.at[i], sem.at[i, 0])

    def write(i):
        return pltpu.make_async_copy(ready.at[i], cuts.at[i], sem_cut.at[i])

    def again(i):
        return pltpu.make_async_copy(ready.at[width + i], cuts.at[tab[i]], sem_cut.at[width + i])

    for i in range(width):
        for copy in load(i):
            copy.start()
    for i in range(width):
        for copy in load(i):
            copy.wait()
        store(i).start()

    def part(i, carry):
        cut(hold, i, ready, i, 0)
        write(i).start()

        @pl.when(tab[i] >= 0)
        def _():
            cut(hold, i, ready, width + i, 1)
            again(i).start()

        return carry

    lax.fori_loop(0, width, part, 0)
    for i in range(width):
        store(i).wait()
        write(i).wait()
        pl.when(tab[i] >= 0)(lambda: again(i).wait())


def send_kernel(start, ways, sent, tab, own, *refs):
    outs, (hold, sem_get, sem_put) = refs[: len(sent)], refs[len(sent) :]
    tile = hold.shape[-1]
    of = [tab[start + ways + way] for way in sent]

    def load(i):
        for c in range(2):
            at = pl.ds(pl.multiple_of(of[i] * tile, tile), tile)
            yield pltpu.make_async_copy(own.at[0, c, :, at], hold.at[i, c], sem_get.at[i, c])

    def store(i):
        return pltpu.make_async_copy(hold.at[i], outs[i], sem_put.at[i])

    for i in range(len(sent)):
        @pl.when(of[i] >= 0)
        def _():
            for copy in load(i):
                copy.start()
    for i in range(len(sent)):
        @pl.when(of[i] >= 0)
        def _():
            for copy in load(i):
                copy.wait()
            store(i).start()
    for i in range(len(sent)):
        pl.when(of[i] >= 0)(lambda: store(i).wait())


def route_kernel(start, ways, taken, sent, slots, tab, *refs):
    got = refs[3 : 3 + len(taken)]
    buf, cuts = refs[3 + len(taken) : 5 + len(taken)]
    outs = refs[6 + len(taken) : 6 + len(taken) + len(sent)]
    hold_in, hold_out, ready, sem_in, sem_out, sem_cut = refs[-6:]

    def load_in(i):
        return pltpu.make_async_copy(got[i], hold_in.at[i], sem_in.at[i])

    def load_out(i, slot):
        return pltpu.make_async_copy(buf.at[slot], hold_out.at[i], sem_out.at[i])

    def store_in(i, slot):
        return pltpu.make_async_copy(hold_in.at[i], buf.at[slot], sem_in.at[i])

    def store_out(i):
        return pltpu.make_async_copy(hold_out.at[i], outs[i], sem_out.at[i])

    def pass_on(i, at):
        return pltpu.make_async_copy(hold_in.at[at], outs[i], sem_out.at[i])

    def write(i, slot):
        return pltpu.make_async_copy(ready.at[i], cuts.at[slot], sem_cut.at[i])

    def again(i):
        at = len(taken) + i
        return pltpu.make_async_copy(ready.at[at], cuts.at[entry(5, taken[i])], sem_cut.at[at])

    def entry(kind, way):
        return tab[start + kind * ways + way]

    to = [entry(0, way) for way in taken]
    of = [entry(1, way) for way in sent]
    keep = [entry(2, way) for way in taken]
    place = [entry(3, way) for way in taken]
    for i, slot in enumerate(of):
        pl.when((slot >= 0) & (slot < slots))(lambda: load_out(i, slot).start())
    for i, slot in enumerate(to):
        pl.when(slot >= 0)(lambda: load_in(i).start())
    for i, slot in enumerate(of):
        @pl.when((slot >= 0) & (slot < slots))
        def _():
            load_out(i, slot).wait()
            store_out(i).start()
    for i, slot in enumerate(to):
        pl.when(slot >= 0)(lambda: load_in(i).wait())
        pl.when(keep[i] >= 0)(lambda: store_in(i, keep[i]).start())
    if taken:
        for i, slot in enumerate(of):
            pl.when(slot >= slots)(lambda: pass_on(i, slot - slots).start())
        for i, way in enumerate(taken):
            @pl.when(place[i] >= 0)
            def _():
                cut(hold_in, i, ready, i, entry(4, way))
                write(i, place[i]).start()

                @pl.when(entry(5, way) >= 0)
                def _():
                    cut(hold_in, i, ready, len(taken) + i, 1 - entry(4, way))
                    again(i).start()
        for i, slot in enumerate(of):
            pl.when(slot >= slots)(lambda: pass_on(i, slot - slots).wait())
    for i, slot in enumerate(of):
        pl.when((slot >= 0) & (slot < slots))(lambda: store_out(i).wait())
    for i in range(len(taken)):
        pl.when(keep[i] >= 0)(lambda: store_in(i, keep[i]).wait())
        pl.when(place[i] >= 0)(lambda: write(i, place[i]).wait())
        pl.when(entry(5, taken[i]) >= 0)(lambda: again(i).wait())


def multiply_kernel(start, first, tab, cuts, *refs):
    if first:
        out, *scratch = refs
        before = None
    else:
        before, out, *scratch = refs
    total, left, right, sem_get, sem_put, sem_l, sem_r = scratch
    tile = cuts.shape[-1]
    count = tab[start]

    def field(i, f):
        return tab[start + 2 + FIELDS * i + f]

    def columns(ref, c, j):
        return ref.at[0, c, :, pl.ds(pl.multiple_of(j * tile, tile), tile)]

    def fetch(i):
        now = lax.rem(i, 2)
        yield pltpu.make_async_copy(cuts.at[field(i, 0)], left.at[now], sem_l.at[now])
        yield pltpu.make_async_copy(cuts.at[field(i, 1)], right.at[now], sem_r.at[now])

    def get(i):
        at = lax.rem(field(i, 5), 2)
        for c in range(2):
            yield pltpu.make_async_copy(columns(before, c, field(i, 2)), total.at[at, c], sem_get.at[2 * at + c])

    def put(group, j):
        at = lax.rem(group, 2)
        for c in range(2):
            yield pltpu.make_async_copy(total.at[at, c], columns(out, c, j), sem_put.at[2 * at + c])

    def begin(i):
        for copy in fetch(i):
            copy.start()

        @pl.when((field(i, 3) > 0) & (field(i, 5) > 1))
        def _():
            for copy in put(field(i, 5), 0):
                copy.wait()

        if not first:
            @pl.when(field(i, 3) == 1)
            def _():
                for copy in get(i):
                    copy.start()

    @pl.when(count > 0)
    def _():
        begin(0)

    def op(i, carry):
        now = lax.rem(i, 2)
        at = lax.rem(field(i, 5), 2)
        if not first:
            @pl.when(field(i, 3) == 1)
            def _():
                for copy in get(i):
                    copy.wait()

        @pl.when(field(i, 3) == 2)
        def _():
            total[at] = jnp.zeros((2, tile, tile), jnp.float32)

        for copy in fetch(i):
            copy.wait()

        @pl.when(i + 1 < count)
        def _():
            begin(i + 1)

        def product(step, carry):
            cl, c = step // 2, lax.rem(step, 2)
            to = cl + c - 2 * cl * c
            sign = (1 - 2 * cl * c).astype(jnp.float32)
            one = jnp.concatenate([left[now, cl, 0], left[now, cl, 0], left[now, cl, 1]], axis=1)
            two = jnp.concatenate([right[now, c, 0], right[now, c, 1], right[now, c, 0]], axis=0)
            total[at, to] += sign * jnp.dot(one, two, preferred_element_type=jnp.float32)
            return carry

        lax.fori_loop(0, 4, product, 0)

        @pl.when(field(i, 4) == 1)
        def _():
            for copy in put(field(i, 5), field(i, 2)):
                copy.start()

        return carry

    lax.fori_loop(0, count, op, 0)
    for back in (2, 1):
        @pl.when(tab[start + 1] >= back)
        def _():
            for copy in put(tab[start + 1] - back, 0):
                copy.wait()


def local(src, rcv, recorded):
    perms, calls, longest, starts, table, slots, places, ways = plan(src, rcv)
    steps = len(perms)
    tile = recorded.shape[2]
    me = lax.axis_index("src") * rcv + lax.axis_index("rcv")
    tab = lax.dynamic_index_in_dim(jnp.asarray(table), me, 0, keepdims=False)
    chunk = jax.ShapeDtypeStruct((2, tile, tile), jnp.float32)
    buf_shape = jax.ShapeDtypeStruct((slots, 2, tile, tile), jnp.float32)
    cut_shape = jax.ShapeDtypeStruct((places, 2, 2, tile, tile), jnp.bfloat16)
    acc_shape = jax.ShapeDtypeStruct(recorded.shape, jnp.float32)
    width = recorded.shape[3] // tile

    def call(kernel, ins, outs, scratch, aliases, cost, limit=None):
        return pl.pallas_call(
            kernel,
            out_shape=outs,
            grid_spec=pltpu.PrefetchScalarGridSpec(
                num_scalar_prefetch=1,
                grid=(),
                in_specs=[ANY] * len(ins),
                out_specs=[ANY] * len(outs),
                scratch_shapes=scratch,
            ),
            input_output_aliases=aliases,
            cost_estimate=pl.CostEstimate(flops=cost[0], bytes_accessed=cost[1], transcendentals=0),
            compiler_params=pltpu.CompilerParams(vmem_limit_bytes=limit),
        )(tab, *ins)

    size = tile * tile * 8
    acc = None
    flight = {}
    own = recorded
    for step in range(min(2, steps)):
        sent = [way for way in range(ways) if perms[step][way]]
        out = call(
            functools.partial(send_kernel, starts["route", step], ways, sent),
            [own],
            [chunk] * len(sent),
            [
                pltpu.VMEM((len(sent), 2, tile, tile), jnp.float32),
                pltpu.SemaphoreType.DMA((len(sent), 2)),
                pltpu.SemaphoreType.DMA((len(sent),)),
            ],
            {},
            (0, 2 * len(sent) * size),
            32 << 20,
        )
        out, own = lax.optimization_barrier((out, own))
        flight[step] = {way: lax.ppermute(value, AXES, perms[step][way]) for way, value in zip(sent, out)}
    buf, cuts = call(
        first_kernel,
        [own],
        [buf_shape, cut_shape],
        [
            pltpu.VMEM((width, 2, tile, tile), jnp.float32),
            pltpu.VMEM((2 * width, 2, 2, tile, tile), jnp.bfloat16),
            pltpu.SemaphoreType.DMA((width, 2)),
            pltpu.SemaphoreType.DMA((2 * width,)),
        ],
        {},
        (0, 3 * width * size),
        48 << 20,
    )
    for step in range(2, steps + 2):
        got = flight.pop(step - 2, {})
        taken = sorted(got)
        sent = [way for way in range(ways) if step < steps and perms[step][way]]
        state = [buf, cuts] if acc is None else [buf, cuts, acc]
        m = len(state)
        kernel = functools.partial(
            route_kernel if m == 3 else first_route, starts["route", step], ways, taken, sent, slots
        )
        done = call(
            kernel,
            state + [got[way] for way in taken],
            [buf_shape, cut_shape, acc_shape][:m] + [chunk] * len(sent),
            [
                pltpu.VMEM((max(len(taken), 1), 2, tile, tile), jnp.float32),
                pltpu.VMEM((max(len(sent), 1), 2, tile, tile), jnp.float32),
                pltpu.VMEM((max(2 * len(taken), 1), 2, 2, tile, tile), jnp.bfloat16),
                pltpu.SemaphoreType.DMA((max(len(taken), 1),)),
                pltpu.SemaphoreType.DMA((max(len(sent), 1),)),
                pltpu.SemaphoreType.DMA((max(2 * len(taken), 1),)),
            ],
            {1 + i: i for i in range(m)},
            (0, (3 * len(taken) + 2 * len(sent)) * size),
            50 << 20,
        )
        buf, cuts = done[:2]
        if m == 3:
            acc = done[2]
        out = done[m:]
        if step in calls and longest[calls.index(step)]:
            ops = longest[calls.index(step)]
            first = acc is None
            (acc,) = call(
                functools.partial(multiply_kernel, starts["ops", step], first),
                [cuts] if first else [cuts, acc],
                [acc_shape],
                [
                    pltpu.VMEM((2, 2, tile, tile), jnp.float32),
                    pltpu.VMEM((2, 2, 2, tile, tile), jnp.bfloat16),
                    pltpu.VMEM((2, 2, 2, tile, tile), jnp.bfloat16),
                    pltpu.SemaphoreType.DMA((4,)),
                    pltpu.SemaphoreType.DMA((4,)),
                    pltpu.SemaphoreType.DMA((2,)),
                    pltpu.SemaphoreType.DMA((2,)),
                ],
                {} if first else {2: 0},
                (ops * 24 * tile**3, ops * 3 * size),
                32 << 20,
            )
            if sent:
                out, acc = lax.optimization_barrier((out, acc))
        flight[step] = {way: lax.ppermute(value, AXES, perms[step][way]) for way, value in zip(sent, out)}
    return acc


def first_route(start, ways, taken, sent, slots, tab, *refs):
    n = 2 + len(taken)
    route_kernel(start, ways, taken, sent, slots, tab, *refs[:2], None, *refs[2 : n + 2], None, *refs[n + 2 :])


def solution(mesh):
    src, rcv = mesh.shape["src"], mesh.shape["rcv"]
    return jax.shard_map(
        functools.partial(local, src, rcv),
        mesh=mesh,
        in_specs=(P("freq", None, "src", "rcv"),),
        out_specs=P("freq", None, "src", "rcv"),
        check_vma=False,
    )
```

```python
import functools
import random

import jax
import jax.numpy as jnp
import numpy as np
from jax import lax
from jax.experimental import pallas as pl
from jax.experimental.pallas import tpu as pltpu
from jax.sharding import PartitionSpec as P

AXES = ("src", "rcv")
FIELDS = 6
CAP = 5


def split_axis(n):
    return (n,) if n <= 4 else (4, n // 4)


class Grid:
    def __init__(self, src, rcv):
        self.src, self.rcv, self.width = src, rcv, src // rcv
        dims = split_axis(src) + split_axis(rcv)
        self.count = src * rcv
        place = np.array(np.unravel_index(np.arange(self.count), dims)).T
        self.dist = np.abs(place[:, None] - place[None]).sum(-1)
        self.ways = []
        for axis, size in enumerate(dims):
            for sign in (1, -1) if size > 2 else (0,):
                pairs = []
                for u in range(self.count):
                    to = place[u].copy()
                    to[axis] = 1 - to[axis] if sign == 0 else to[axis] + sign
                    if 0 <= to[axis] < size:
                        pairs.append((u, int(np.ravel_multi_index(tuple(to), dims))))
                if pairs:
                    self.ways.append(pairs)
        self.tiles = [(p, q) for p in range(src) for q in range(p, src)]
        self.number = {}
        for i, (p, q) in enumerate(self.tiles):
            self.number[p, q] = self.number[q, p] = i

    def columns(self, x):
        return range(x * self.width, (x + 1) * self.width)


def plan_moves(grid, seed):
    rnd = random.Random(seed)
    items, n = len(grid.tiles), grid.count
    has = np.full((n, items), 10**6)
    need = np.zeros((n, items), bool)
    row = np.zeros((n, items), bool)
    flip = np.zeros((n, items), bool)
    for d in range(n):
        s, x = divmod(d, grid.rcv)
        for q in range(grid.src):
            need[d, grid.number[s, q]] = True
            row[d, grid.number[s, q]] = True
            for j in grid.columns(x):
                need[d, grid.number[q, j]] = True
        for q in grid.columns(x):
            has[d, grid.number[s, q]] = 0
            flip[d, grid.number[s, q]] = s > q
    links = [(way, u, v) for way, pairs in enumerate(grid.ways) for u, v in pairs]
    degree = np.zeros(n)
    for _, _, v in links:
        degree[v] += 1
    near = np.stack([grid.dist[has[:, i] == 0].min(0) for i in range(items)])
    moves, step = [], 0
    while True:
        missing = need & (has > 10**5)
        if not missing.any():
            return moves, has, flip
        load = missing.sum(1) / degree
        weight = missing.sum(1) / np.maximum(need.sum(1), 1)
        rnd.shuffle(links)
        links.sort(key=lambda link: -load[link[2]])
        open_ = has > 10**5
        into = [[] for _ in range(n)]
        for _, u, v in links:
            into[v].append(u)
        ready = has <= step
        now = []
        for way, u, v in links:
            cand = np.nonzero(ready[u] & open_[v])[0]
            if not len(cand):
                continue
            helped = (missing[:, cand].T & (grid.dist[v][None] < near[cand])).astype(float)
            helped[:, v] = 0
            value = 3.0 * missing[v, cand] + helped @ weight
            useful = value > 0
            if not useful.any():
                continue
            others = sum(ready[w, cand].astype(float) for w in into[v])
            value = value + 0.5 * np.array([rnd.random() for _ in cand]) - 0.7 * (others - 1)
            value = value + 3.0 * (row[v, cand] & missing[v, cand])
            value[~useful] = -100
            item = int(cand[np.argmax(value)])
            open_[v, item] = False
            missing[v, item] = False
            near[item] = np.minimum(near[item], grid.dist[v])
            now.append((way, u, v, item))
        for _, u, v, item in now:
            has[v, item] = step + 2
            flip[v, item] = flip[u, item]
        moves.append(now)
        step += 1


def plan_products(grid, moves, has, flip):
    steps, n = len(moves), grid.count
    calls = [*range(3, steps + 2)]
    lists = [[[] for _ in range(n)] for _ in calls]
    for d in range(n):
        s, x = divmod(d, grid.rcv)
        todo = []
        for k in range(grid.src):
            left = grid.number[s, k]
            for j, q in enumerate(grid.columns(x)):
                right = grid.number[k, q]
                todo.append((max(has[d, left], has[d, right]), k, j, left, right, q))
        todo.sort()
        for at, step in enumerate(calls):
            fit = [one for one in todo if one[0] <= step]
            if step < steps + 1:
                alike = {j: sum(one[2] == j for one in fit) for j in range(grid.width)}
                fit.sort(key=lambda one: (-alike[one[2]], one[2], one[0]))
                fit = fit[:CAP]
            fit.sort(key=lambda one: (one[2], one[0]))
            todo = [one for one in todo if one not in fit]
            lists[at][d] = [one[1:] for one in fit]
        assert not todo
    return calls, lists


@functools.lru_cache(None)
def plan(src, rcv):
    grid = Grid(src, rcv)
    best = None
    for seed in range(240 if grid.count <= 16 else 1):
        got = plan_moves(grid, seed)
        calls, work = plan_products(grid, *got)
        late = [max(len(per) for per in lists) for lists in work[-3:]]
        cost = 46 * len(got[0]) + 4 * (late[2] + max(late[1] - 5, 0) + max(late[0] - 5, 0))
        if best is None or cost < best[0]:
            best = cost, got, calls, work
    (moves, has, flip), calls, work = best[1:]
    n, ways, steps = grid.count, len(grid.ways), len(moves)
    slot = np.full((n, len(grid.tiles)), -1)
    used = np.zeros(n, int)
    for d in range(n):
        s, x = divmod(d, rcv)
        for q in grid.columns(x):
            slot[d, grid.number[s, q]] = used[d]
            used[d] += 1
    keep = np.zeros((n, len(grid.tiles)), bool)
    for step, now in enumerate(moves):
        for way, u, v, item in now:
            keep[u, item] |= has[u, item] < step
    send = np.full((steps + 2, ways, n), -1)
    take = np.full((steps + 2, ways, n), -1)
    turn = np.zeros((steps + 2, ways, n), int)
    use = np.zeros((n, len(grid.tiles)), bool)
    rows = np.zeros((n, len(grid.tiles)), int)
    for d in range(n):
        s, x = divmod(d, rcv)
        for i in range(len(grid.tiles)):
            p, q = grid.tiles[i]
            rows[d, i] = s if s in (p, q) else p if q in grid.columns(x) else q
            use[d, i] = s in (p, q) or p in grid.columns(x) or q in grid.columns(x)
    place = slot.copy()
    other = np.full((n, len(grid.tiles)), -1)
    placed = used.copy()
    both = np.zeros((n, len(grid.tiles)), bool)
    for d in range(n):
        for i in range(len(grid.tiles)):
            p, q = grid.tiles[i]
            s, at = d // rcv, grid.columns(d % rcv)
            both[d, i] = p != q and (p in at and q in at or s in (p, q) and s in at)
            if place[d, i] >= 0 and both[d, i]:
                other[d, i] = placed[d]
                placed[d] += 1
    perms = [[[] for _ in range(ways)] for _ in range(steps)]
    for step, now in enumerate(moves):
        for way, u, v, item in now:
            if keep[v, item]:
                slot[v, item] = used[v]
                used[v] += 1
            take[step + 2, way, v] = item
            if use[v, item]:
                place[v, item] = placed[v]
                placed[v] += 1
                if both[v, item]:
                    other[v, item] = placed[v]
                    placed[v] += 1
                p, q = grid.tiles[item]
                turn[step + 2, way, v] = int(p != q and (rows[v, item] == q) != flip[v, item])
            perms[step][way].append((u, v))
    for step, now in enumerate(moves):
        taken = [way for way in range(ways) if step >= 2 and perms[step - 2][way]]
        for way, u, v, item in now:
            new = [i for i, w in enumerate(taken) if take[step, w, u] == item]
            send[step, way, u] = used.max() + new[0] if new else slot[u, item]
    kept = np.full((steps + 2, ways, n), -1)
    store = np.full((steps + 2, ways, n), -1)
    again = np.full((steps + 2, ways, n), -1)
    for step, now in enumerate(moves):
        for way, u, v, item in now:
            kept[step + 2, way, v] = slot[v, item]
            store[step + 2, way, v] = place[v, item]
            again[step + 2, way, v] = other[v, item]
    lists = [[[] for _ in range(n)] for _ in calls]
    fresh = [set() for _ in range(n)]
    for at, per in enumerate(work):
        for d in range(n):
            s = d // rcv
            for i, (k, j, left, right, q) in enumerate(per[d]):
                begin = i == 0 or per[d][i - 1][1] != j
                end = i + 1 == len(per[d]) or per[d][i + 1][1] != j
                over = other[d, right] if k != q and rows[d, right] != k else place[d, right]
                assert over >= 0
                mode = 0 if not begin else 1 if j in fresh[d] else 2
                fresh[d].add(j)
                group = len({one[1] for one in per[d][: i + 1]}) - 1
                lists[at][d].append((place[d, left], over, j, mode, int(end), group))
    longest = [max(len(one) for one in per) for per in lists]
    table = []
    starts = {"own": 0}
    for q in range(grid.width):
        table.append(np.array([other[d, grid.number[d // rcv, d % rcv * grid.width + q]] for d in range(n)]))
    for step in range(steps + 2):
        starts["route", step] = len(table)
        for what in (take, send, kept, store, turn, again):
            for way in range(ways):
                table.append(what[step, way])
    for at, step in enumerate(calls):
        starts["ops", step] = len(table)
        table.append(np.array([len(lists[at][d]) for d in range(n)]))
        table.append(np.array([lists[at][d][-1][5] + 1 if lists[at][d] else 0 for d in range(n)]))
        for i in range(longest[at]):
            for f in range(FIELDS):
                table.append(np.array([lists[at][d][i][f] if i < len(lists[at][d]) else 0 for d in range(n)]))
    return perms, calls, longest, starts, np.array(table, np.int32).T.copy(), int(used.max()), int(placed.max()), ways


ANY = pl.BlockSpec(memory_space=pl.ANY)


def split(value):
    high = value.astype(jnp.bfloat16)
    return high, (value - high.astype(jnp.float32)).astype(jnp.bfloat16)


def cut(ref, at, out, to, turn):
    tile = ref.shape[-1]
    rows = min(128, tile)
    count = tile // rows

    def block(r):
        return pl.ds(pl.multiple_of(r * rows, rows), rows)

    def straight(i, carry):
        c, r = i // count, lax.rem(i, count)
        out[to, c, 0, block(r), :], out[to, c, 1, block(r), :] = split(ref[at, c, block(r), :])
        return carry

    def across(i, carry):
        c, r = i // count, lax.rem(i, count)
        out[to, c, 0, block(r), :], out[to, c, 1, block(r), :] = split(ref[at, c, :, block(r)].T)
        return carry

    @pl.when(turn == 0)
    def _():
        lax.fori_loop(0, 2 * count, straight, 0)

    @pl.when(turn != 0)
    def _():
        lax.fori_loop(0, 2 * count, across, 0)


def first_kernel(tab, own, buf, cuts, hold, ready, sem, sem_cut):
    tile = buf.shape[-1]
    width = own.shape[-1] // tile

    def load(i):
        for c in range(2):
            yield pltpu.make_async_copy(own.at[0, c, :, pl.ds(i * tile, tile)], hold.at[i, c], sem.at[i, c])

    def store(i):
        return pltpu.make_async_copy(hold.at[i], buf.at[i], sem.at[i, 0])

    def write(i):
        return pltpu.make_async_copy(ready.at[i], cuts.at[i], sem_cut.at[i])

    def again(i):
        return pltpu.make_async_copy(ready.at[width + i], cuts.at[tab[i]], sem_cut.at[width + i])

    for i in range(width):
        for copy in load(i):
            copy.start()
    for i in range(width):
        for copy in load(i):
            copy.wait()
        store(i).start()

    def part(i, carry):
        cut(hold, i, ready, i, 0)
        write(i).start()

        @pl.when(tab[i] >= 0)
        def _():
            cut(hold, i, ready, width + i, 1)
            again(i).start()

        return carry

    lax.fori_loop(0, width, part, 0)
    for i in range(width):
        store(i).wait()
        write(i).wait()
        pl.when(tab[i] >= 0)(lambda: again(i).wait())


def send_kernel(start, ways, sent, tab, own, *refs):
    outs, (hold, sem_get, sem_put) = refs[: len(sent)], refs[len(sent) :]
    tile = hold.shape[-1]
    of = [tab[start + ways + way] for way in sent]

    def load(i):
        for c in range(2):
            at = pl.ds(pl.multiple_of(of[i] * tile, tile), tile)
            yield pltpu.make_async_copy(own.at[0, c, :, at], hold.at[i, c], sem_get.at[i, c])

    def store(i):
        return pltpu.make_async_copy(hold.at[i], outs[i], sem_put.at[i])

    for i in range(len(sent)):
        @pl.when(of[i] >= 0)
        def _():
            for copy in load(i):
                copy.start()
    for i in range(len(sent)):
        @pl.when(of[i] >= 0)
        def _():
            for copy in load(i):
                copy.wait()
            store(i).start()
    for i in range(len(sent)):
        pl.when(of[i] >= 0)(lambda: store(i).wait())


def route_kernel(start, ways, taken, sent, slots, tab, *refs):
    got = refs[3 : 3 + len(taken)]
    buf, cuts = refs[3 + len(taken) : 5 + len(taken)]
    outs = refs[6 + len(taken) : 6 + len(taken) + len(sent)]
    hold_in, hold_out, ready, sem_in, sem_out, sem_cut = refs[-6:]

    def load_in(i):
        return pltpu.make_async_copy(got[i], hold_in.at[i], sem_in.at[i])

    def load_out(i, slot):
        return pltpu.make_async_copy(buf.at[slot], hold_out.at[i], sem_out.at[i])

    def store_in(i, slot):
        return pltpu.make_async_copy(hold_in.at[i], buf.at[slot], sem_in.at[i])

    def store_out(i):
        return pltpu.make_async_copy(hold_out.at[i], outs[i], sem_out.at[i])

    def pass_on(i, at):
        return pltpu.make_async_copy(hold_in.at[at], outs[i], sem_out.at[i])

    def write(i, slot):
        return pltpu.make_async_copy(ready.at[i], cuts.at[slot], sem_cut.at[i])

    def again(i):
        at = len(taken) + i
        return pltpu.make_async_copy(ready.at[at], cuts.at[entry(5, taken[i])], sem_cut.at[at])

    def entry(kind, way):
        return tab[start + kind * ways + way]

    to = [entry(0, way) for way in taken]
    of = [entry(1, way) for way in sent]
    keep = [entry(2, way) for way in taken]
    place = [entry(3, way) for way in taken]
    for i, slot in enumerate(of):
        pl.when((slot >= 0) & (slot < slots))(lambda: load_out(i, slot).start())
    for i, slot in enumerate(to):
        pl.when(slot >= 0)(lambda: load_in(i).start())
    for i, slot in enumerate(of):
        @pl.when((slot >= 0) & (slot < slots))
        def _():
            load_out(i, slot).wait()
            store_out(i).start()
    for i, slot in enumerate(to):
        pl.when(slot >= 0)(lambda: load_in(i).wait())
        pl.when(keep[i] >= 0)(lambda: store_in(i, keep[i]).start())
    if taken:
        for i, slot in enumerate(of):
            pl.when(slot >= slots)(lambda: pass_on(i, slot - slots).start())
        for i, way in enumerate(taken):
            @pl.when(place[i] >= 0)
            def _():
                cut(hold_in, i, ready, i, entry(4, way))
                write(i, place[i]).start()

                @pl.when(entry(5, way) >= 0)
                def _():
                    cut(hold_in, i, ready, len(taken) + i, 1 - entry(4, way))
                    again(i).start()
        for i, slot in enumerate(of):
            pl.when(slot >= slots)(lambda: pass_on(i, slot - slots).wait())
    for i, slot in enumerate(of):
        pl.when((slot >= 0) & (slot < slots))(lambda: store_out(i).wait())
    for i in range(len(taken)):
        pl.when(keep[i] >= 0)(lambda: store_in(i, keep[i]).wait())
        pl.when(place[i] >= 0)(lambda: write(i, place[i]).wait())
        pl.when(entry(5, taken[i]) >= 0)(lambda: again(i).wait())


def multiply_kernel(start, first, tab, cuts, *refs):
    if first:
        out, *scratch = refs
        before = None
    else:
        before, out, *scratch = refs
    total, left, right, sem_get, sem_put, sem_l, sem_r = scratch
    tile = cuts.shape[-1]
    count = tab[start]

    def field(i, f):
        return tab[start + 2 + FIELDS * i + f]

    def columns(ref, c, j):
        return ref.at[0, c, :, pl.ds(pl.multiple_of(j * tile, tile), tile)]

    def fetch(i):
        now = lax.rem(i, 2)
        yield pltpu.make_async_copy(cuts.at[field(i, 0)], left.at[now], sem_l.at[now])
        yield pltpu.make_async_copy(cuts.at[field(i, 1)], right.at[now], sem_r.at[now])

    def get(i):
        at = lax.rem(field(i, 5), 2)
        for c in range(2):
            yield pltpu.make_async_copy(columns(before, c, field(i, 2)), total.at[at, c], sem_get.at[2 * at + c])

    def put(group, j):
        at = lax.rem(group, 2)
        for c in range(2):
            yield pltpu.make_async_copy(total.at[at, c], columns(out, c, j), sem_put.at[2 * at + c])

    def begin(i):
        for copy in fetch(i):
            copy.start()

        @pl.when((field(i, 3) > 0) & (field(i, 5) > 1))
        def _():
            for copy in put(field(i, 5), 0):
                copy.wait()

        if not first:
            @pl.when(field(i, 3) == 1)
            def _():
                for copy in get(i):
                    copy.start()

    @pl.when(count > 0)
    def _():
        begin(0)

    def op(i, carry):
        now = lax.rem(i, 2)
        at = lax.rem(field(i, 5), 2)
        if not first:
            @pl.when(field(i, 3) == 1)
            def _():
                for copy in get(i):
                    copy.wait()

        @pl.when(field(i, 3) == 2)
        def _():
            total[at] = jnp.zeros((2, tile, tile), jnp.float32)

        for copy in fetch(i):
            copy.wait()

        @pl.when(i + 1 < count)
        def _():
            begin(i + 1)

        def product(step, carry):
            cl, c = step // 2, lax.rem(step, 2)
            to = cl + c - 2 * cl * c
            sign = (1 - 2 * cl * c).astype(jnp.float32)
            one = jnp.concatenate([left[now, cl, 0], left[now, cl, 0], left[now, cl, 1]], axis=1)
            two = jnp.concatenate([right[now, c, 0], right[now, c, 1], right[now, c, 0]], axis=0)
            total[at, to] += sign * jnp.dot(one, two, preferred_element_type=jnp.float32)
            return carry

        lax.fori_loop(0, 4, product, 0)

        @pl.when(field(i, 4) == 1)
        def _():
            for copy in put(field(i, 5), field(i, 2)):
                copy.start()

        return carry

    lax.fori_loop(0, count, op, 0)
    for back in (2, 1):
        @pl.when(tab[start + 1] >= back)
        def _():
            for copy in put(tab[start + 1] - back, 0):
                copy.wait()


def local(src, rcv, recorded):
    perms, calls, longest, starts, table, slots, places, ways = plan(src, rcv)
    steps = len(perms)
    tile = recorded.shape[2]
    me = lax.axis_index("src") * rcv + lax.axis_index("rcv")
    tab = lax.dynamic_index_in_dim(jnp.asarray(table), me, 0, keepdims=False)
    chunk = jax.ShapeDtypeStruct((2, tile, tile), jnp.float32)
    buf_shape = jax.ShapeDtypeStruct((slots, 2, tile, tile), jnp.float32)
    cut_shape = jax.ShapeDtypeStruct((places, 2, 2, tile, tile), jnp.bfloat16)
    acc_shape = jax.ShapeDtypeStruct(recorded.shape, jnp.float32)
    width = recorded.shape[3] // tile

    def call(kernel, ins, outs, scratch, aliases, cost, limit=None):
        return pl.pallas_call(
            kernel,
            out_shape=outs,
            grid_spec=pltpu.PrefetchScalarGridSpec(
                num_scalar_prefetch=1,
                grid=(),
                in_specs=[ANY] * len(ins),
                out_specs=[ANY] * len(outs),
                scratch_shapes=scratch,
            ),
            input_output_aliases=aliases,
            cost_estimate=pl.CostEstimate(flops=cost[0], bytes_accessed=cost[1], transcendentals=0),
            compiler_params=pltpu.CompilerParams(vmem_limit_bytes=limit),
        )(tab, *ins)

    size = tile * tile * 8
    acc = None
    flight = {}
    own = recorded
    for step in range(min(2, steps)):
        sent = [way for way in range(ways) if perms[step][way]]
        out = call(
            functools.partial(send_kernel, starts["route", step], ways, sent),
            [own],
            [chunk] * len(sent),
            [
                pltpu.VMEM((len(sent), 2, tile, tile), jnp.float32),
                pltpu.SemaphoreType.DMA((len(sent), 2)),
                pltpu.SemaphoreType.DMA((len(sent),)),
            ],
            {},
            (0, 2 * len(sent) * size),
            32 << 20,
        )
        out, own = lax.optimization_barrier((out, own))
        flight[step] = {way: lax.ppermute(value, AXES, perms[step][way]) for way, value in zip(sent, out)}
    buf, cuts = call(
        first_kernel,
        [own],
        [buf_shape, cut_shape],
        [
            pltpu.VMEM((width, 2, tile, tile), jnp.float32),
            pltpu.VMEM((2 * width, 2, 2, tile, tile), jnp.bfloat16),
            pltpu.SemaphoreType.DMA((width, 2)),
            pltpu.SemaphoreType.DMA((2 * width,)),
        ],
        {},
        (0, 3 * width * size),
        48 << 20,
    )
    for step in range(2, steps + 2):
        got = flight.pop(step - 2, {})
        taken = sorted(got)
        sent = [way for way in range(ways) if step < steps and perms[step][way]]
        state = [buf, cuts] if acc is None else [buf, cuts, acc]
        m = len(state)
        kernel = functools.partial(
            route_kernel if m == 3 else first_route, starts["route", step], ways, taken, sent, slots
        )
        done = call(
            kernel,
            state + [got[way] for way in taken],
            [buf_shape, cut_shape, acc_shape][:m] + [chunk] * len(sent),
            [
                pltpu.VMEM((max(len(taken), 1), 2, tile, tile), jnp.float32),
                pltpu.VMEM((max(len(sent), 1), 2, tile, tile), jnp.float32),
                pltpu.VMEM((max(2 * len(taken), 1), 2, 2, tile, tile), jnp.bfloat16),
                pltpu.SemaphoreType.DMA((max(len(taken), 1),)),
                pltpu.SemaphoreType.DMA((max(len(sent), 1),)),
                pltpu.SemaphoreType.DMA((max(2 * len(taken), 1),)),
            ],
            {1 + i: i for i in range(m)},
            (0, (3 * len(taken) + 2 * len(sent)) * size),
            50 << 20,
        )
        buf, cuts = done[:2]
        if m == 3:
            acc = done[2]
        out = done[m:]
        if step in calls and longest[calls.index(step)]:
            ops = longest[calls.index(step)]
            first = acc is None
            (acc,) = call(
                functools.partial(multiply_kernel, starts["ops", step], first),
                [cuts] if first else [cuts, acc],
                [acc_shape],
                [
                    pltpu.VMEM((2, 2, tile, tile), jnp.float32),
                    pltpu.VMEM((2, 2, 2, tile, tile), jnp.bfloat16),
                    pltpu.VMEM((2, 2, 2, tile, tile), jnp.bfloat16),
                    pltpu.SemaphoreType.DMA((4,)),
                    pltpu.SemaphoreType.DMA((4,)),
                    pltpu.SemaphoreType.DMA((2,)),
                    pltpu.SemaphoreType.DMA((2,)),
                ],
                {} if first else {2: 0},
                (ops * 24 * tile**3, ops * 3 * size),
                32 << 20,
            )
            if sent:
                out, acc = lax.optimization_barrier((out, acc))
        flight[step] = {way: lax.ppermute(value, AXES, perms[step][way]) for way, value in zip(sent, out)}
    return acc


def first_route(start, ways, taken, sent, slots, tab, *refs):
    n = 2 + len(taken)
    route_kernel(start, ways, taken, sent, slots, tab, *refs[:2], None, *refs[2 : n + 2], None, *refs[n + 2 :])


def solution(mesh):
    src, rcv = mesh.shape["src"], mesh.shape["rcv"]
    return jax.shard_map(
        functools.partial(local, src, rcv),
        mesh=mesh,
        in_specs=(P("freq", None, "src", "rcv"),),
        out_specs=P("freq", None, "src", "rcv"),
        check_vma=False,
    )
```
